32 devices in a mesh: row: 4 (over y, x), col: 4 (over z), depth: 2 (over core).
Axes of the slice: x: 2, y: 2, z: 4, core: 2. Of those that a mesh axis runs over, the one named last changes fastest.
Arguments:
- blocks: bfloat16 [128, 12, 128, 128], P(('row', 'col'), None, 'depth'), may hold values from -0.5 to 0.5
- cols: int32 [128, 12], replicated, may hold values from -1 to 127, as said below
- res: int32 [128, 12], replicated, may hold values from 0 to 127, as said below
Outputs:
- purified: bfloat16 [128, 12, 128, 128], P(('row', 'col'), None, None, 'depth')
The draws below stay inside these ranges and needn't reach their ends.
Inputs may be any that keep to these rules, and one draw needn't show every extreme that they name: `cols`: slots 0 to c-1 of block row i hold distinct columns (i + o) mod 128 with |o| <= 8, slot 0 being i itself; the count c lies between 6 and 12, varies by row, and both ends are reached; the remaining slots hold -1. `res`: block row i keeps 12 distinct columns (i + o) mod 128 with |o| <= 8, the first being i.
All inputs are finite; a program needn't handle non-finite values.
Results may differ from the reference program's by a relative error of at most 0.0044.
Values may be sent and summed in bfloat16 or wider, within the bound.
A program may use at most 64 MiB of HBM per device.

```python
import jax
import jax.numpy as jnp
from jax import lax

B = 128
K = 12
R = 12
W = 8
NB = 128


def band_offsets(key, count):
    width_all = 2 * W + 1
    places = jnp.arange(width_all, dtype=jnp.int32)
    scores = jax.random.randint(key, (NB, width_all), 1, 1 << 20, dtype=jnp.int32) * width_all + places[None, :]
    scores = jnp.where(places[None, :] == W, 0, scores)
    order = jnp.argsort(scores, axis=1, stable=True).astype(jnp.int32)
    return order[:, :count] - W


def draw_cols(key, part):
    offsets = band_offsets(jax.random.fold_in(key, 11), K)
    row_ids = jnp.arange(NB, dtype=jnp.int32)
    columns = (row_ids[:, None] + offsets) % NB
    counts = jax.random.randint(jax.random.fold_in(key, 12), (NB,), K // 2, K + 1, dtype=jnp.int32)
    counts = jnp.where(row_ids == 0, K, counts)
    counts = jnp.where(row_ids == 1, K // 2, counts)
    present = jnp.arange(K, dtype=jnp.int32)[None, :] < counts[:, None]
    return jnp.where(present, columns, -1).astype(jnp.int32)


def draw_res(key, part):
    offsets = band_offsets(jax.random.fold_in(key, 13), R)
    row_ids = jnp.arange(NB, dtype=jnp.int32)
    return ((row_ids[:, None] + offsets) % NB).astype(jnp.int32)


def block_levels(rng, dims, pieces, low, high):
    gain, own = 1.0, jax.random.fold_in(rng, 6)
    for position, parts in pieces:
        steps = jnp.exp(jax.random.uniform(jax.random.fold_in(own, position), (parts,), jnp.float32, low / len(pieces), high / len(pieces)))
        gain = gain * jnp.repeat(steps, dims[position] // parts).reshape([-1 if axis == position else 1 for axis in range(len(dims))])
    return gain


def noise(key, shape, width, most, cuts=(), held_as=jnp.bfloat16):
    entries = jax.random.normal(key, shape, jnp.float32) * width
    if len(cuts) > 0:
        entries = block_levels(key, shape, cuts, -0.22, 0.18) * entries
    return jnp.clip(entries, min=-most, max=most).astype(held_as)


def setup_inputs(seed: int = 0) -> dict:
    splits = jax.random.split(jax.random.key(seed), 4)
    return {
        "blocks": noise(splits[0], (NB, K, B, B), B ** -0.5, 0.5, ((0, 16), (2, 2))),
        "cols": draw_cols(jax.random.fold_in(splits[3], 71), 0),
        "res": draw_res(jax.random.fold_in(splits[3], 71), 0),
    }


def find_tiles(blocks, cols, source, target):
    present = source >= 0
    source_row = jnp.where(present, source, 0).astype(jnp.int32)
    listed = cols[source_row]
    matches = listed == target[..., None]
    slot_index = jnp.sum(jnp.where(matches, jnp.arange(listed.shape[-1], dtype=jnp.int32), 0), axis=-1).astype(jnp.int32)
    usable = present & jnp.any(matches, axis=-1)
    tiles = blocks[source_row, slot_index].astype(jnp.float32)
    return jnp.where(usable[..., None, None], tiles, jnp.zeros_like(tiles))


def reference(blocks, cols, res):
    def one_row(block_row):
        own_cols = cols[block_row]
        own_res = res[block_row]
        right_first = find_tiles(blocks, cols, own_cols[:, None], own_res[None, :])
        square = jnp.einsum("sab,sqbc->qac", blocks[block_row].astype(jnp.float32), right_first)
        rounded = lax.optimization_barrier(square.astype(jnp.bfloat16)).astype(jnp.float32)
        right_second = find_tiles(blocks, cols, own_res[:, None], own_res[None, :])
        cube = jnp.einsum("qab,qrbc->rac", rounded, right_second)
        return (3.0 * square - 2.0 * cube).astype(jnp.bfloat16)

    return lax.map(one_row, jnp.arange(cols.shape[0], dtype=jnp.int32))
```

```python
import functools

import jax
import jax.numpy as jnp
from jax import lax
from jax.experimental import pallas as pl
from jax.experimental.pallas import tpu as pltpu
from jax.sharding import PartitionSpec as P

W = 8
ROWS = 8
LANES = 128
MESH = pl.DeviceIdType.MESH
OWN_COLS, OWN_RES, UP_SLOT, DOWN_SLOT, COUNT, META_ROWS = 40, 56, 72, 88, 104, 112


def group_index():
    return lax.axis_index("row") * lax.axis_size("col") + lax.axis_index("col")


def index_kernel(cols_ref, res_ref, meta_ref):
    slots, count = cols_ref.shape
    cols = cols_ref[...]
    res = res_ref[...]
    row = lax.broadcasted_iota(jnp.int32, (slots, count), 1)
    half = count // 2

    def offset(values):
        t = values - row
        t = jnp.where(t > half, t - count, t)
        return jnp.where(t < -half, t + count, t)

    present = cols >= 0
    off = offset(cols)
    in_group = row & (ROWS - 1)
    lane_group = in_group[:1]
    need_up = present & (in_group + off >= 0)
    need_down = present & (in_group + off <= ROWS - 1)

    def positions(need):
        ones = jnp.where(need, 1, 0)
        run = jnp.zeros((1, count), jnp.int32)
        within = []
        for s in range(slots):
            within.append(run)
            run = run + ones[s : s + 1]
        before = jnp.zeros((1, count), jnp.int32)
        wide = jnp.broadcast_to(run, (8, count))
        for j in range(1, ROWS):
            before = before + jnp.where(lane_group >= j, pltpu.roll(wide, j, 1)[:1], 0)
        return jnp.concatenate([w + before for w in within], axis=0), before + run

    pos_up, total_up = positions(need_up)
    pos_down, total_down = positions(need_down)
    most = jnp.max(jnp.maximum(total_up, total_down))

    first = group_index() * ROWS
    shift = lax.rem(count - first + ROWS, count)

    def window(values):
        padded = jnp.concatenate(
            [values, jnp.zeros((16 - slots, count), jnp.int32)], axis=0
        )
        return pltpu.roll(padded, shift, 1)[:, :LANES]

    span = ROWS * slots
    empty = 3 * span
    lane = lax.broadcasted_iota(jnp.int32, (16, LANES), 1)
    slot = lax.broadcasted_iota(jnp.int32, (16, LANES), 0)
    up_slot = window(jnp.where(need_up, pos_up, span))
    down_slot = window(jnp.where(need_down, pos_down, span))
    off_w = window(jnp.where(present, off, 4 * W))
    here = off_w < 4 * W
    place = jnp.where(
        lane < ROWS,
        jnp.where(up_slot < span, span + up_slot, empty),
        jnp.where(
            lane < 2 * ROWS,
            (lane - ROWS) * slots + slot,
            jnp.where(down_slot < span, 2 * span + down_slot, empty),
        ),
    )
    place = jnp.where(here & (lane < 3 * ROWS), place, empty)
    wanted = lax.broadcasted_iota(jnp.int32, (OWN_COLS, LANES), 0) - 2 * W
    dense = jnp.full((OWN_COLS, LANES), empty, jnp.int32)
    for s in range(slots):
        dense = jnp.where(off_w[s : s + 1] == wanted, place[s : s + 1], dense)
    meta_ref[:OWN_COLS] = dense
    reach_col = off_w + lane
    meta_ref[OWN_COLS:OWN_RES] = jnp.where(
        here, (2 * W - reach_col) * LANES + reach_col, LANES - 1
    )
    meta_ref[OWN_RES:UP_SLOT] = window(offset(res)) + lane
    meta_ref[UP_SLOT:DOWN_SLOT] = up_slot
    meta_ref[DOWN_SLOT:COUNT] = down_slot
    meta_ref[COUNT:] = jnp.full((META_ROWS - COUNT, LANES), most, jnp.int32)


def pack_kernel(slots, meta_ref, blocks_ref, up_ref, down_ref):
    for u in range(ROWS):

        @pl.loop(0, slots)
        def _(s):
            block = blocks_ref[u * slots + s]
            up_ref[meta_ref[(UP_SLOT + s) * LANES + ROWS + u]] = block
            down_ref[meta_ref[(DOWN_SLOT + s) * LANES + ROWS + u]] = block


def step_kernel(
    cap,
    chunks,
    slots,
    kept,
    meta_ref,
    blocks_ref,
    up_ref,
    down_ref,
    out_ref,
    table,
    square,
    rounded,
    outgoing,
    own_sem,
    send_sem,
    recv_sem,
    pass_send_sem,
    pass_recv_sem,
    out_send_sem,
    out_recv_sem,
):
    row, col, depth = (lax.axis_index(a) for a in ("row", "col", "depth"))
    row_count, col_count = lax.axis_size("row"), lax.axis_size("col")
    groups = row_count * col_count
    group = row * col_count + col
    following = lax.rem(group + 1, groups)
    preceding = lax.rem(group + groups - 1, groups)
    sibling = (row, col, 1 - depth)
    after = (following // col_count, lax.rem(following, col_count), depth)
    before = (preceding // col_count, lax.rem(preceding, col_count), depth)

    barrier = pltpu.get_barrier_semaphore()
    for device in (sibling, after, before):
        pl.semaphore_signal(barrier, inc=1, device_id=device, device_id_type=MESH)
    pl.semaphore_wait(barrier, 3)

    span = ROWS * slots
    part = cap // chunks
    edge = blocks_ref.shape[1]
    mine = pl.ds(pl.multiple_of(depth * edge, edge), edge)

    halo = []
    for c in range(chunks):
        for way, (source, device) in enumerate(((up_ref, after), (down_ref, before))):
            start = span * (way + 1) + c * part
            k = 2 * c + way
            copy = pltpu.make_async_remote_copy(
                src_ref=source.at[pl.ds(c * part, part)],
                dst_ref=table.at[pl.ds(start, part), mine, :],
                send_sem=send_sem.at[k],
                recv_sem=recv_sem.at[k],
                device_id=device,
                device_id_type=MESH,
            )
            copy.start()
            halo.append((k, start, copy))
    keep = pltpu.make_async_copy(
        blocks_ref, table.at[pl.ds(0, span), mine, :], own_sem.at[0]
    )
    keep.start()
    share = pltpu.make_async_remote_copy(
        src_ref=blocks_ref,
        dst_ref=table.at[pl.ds(0, span), mine, :],
        send_sem=own_sem.at[1],
        recv_sem=own_sem.at[2],
        device_id=sibling,
        device_id_type=MESH,
    )
    share.start()
    table[3 * span] = jnp.zeros(table.shape[1:], table.dtype)
    passed = []
    for k, start, copy in halo:
        copy.wait_recv()
        forward = pltpu.make_async_remote_copy(
            src_ref=table.at[pl.ds(start, part), mine, :],
            dst_ref=table.at[pl.ds(start, part), mine, :],
            send_sem=pass_send_sem.at[k],
            recv_sem=pass_recv_sem.at[k],
            device_id=sibling,
            device_id_type=MESH,
        )
        forward.start()
        passed.append(forward)
    keep.wait()
    share.wait()
    for forward in passed:
        forward.wait()
    for _, _, copy in halo:
        copy.wait_send()

    rows_here = ROWS // 2
    size = table.shape[2]
    lane = lax.broadcasted_iota(jnp.int32, (size, size), 1)
    low = lane < size // 2
    even = depth == 0

    def right(base0, base1, to0, to1):
        return jnp.concatenate(
            [
                jnp.concatenate(
                    [table[meta_ref[b + to0]], table[meta_ref[b + to1]]], axis=1
                )
                for b in (base0, base1)
            ],
            axis=0,
        )

    def send_row(r):
        return pltpu.make_async_remote_copy(
            src_ref=outgoing.at[r],
            dst_ref=out_ref.at[depth * rows_here + r],
            send_sem=out_send_sem.at[r],
            recv_sem=out_recv_sem.at[r],
            device_id=sibling,
            device_id_type=MESH,
        )

    @pl.loop(0, rows_here)
    def _(r):
        i = depth * rows_here + r

        @pl.loop(0, kept // 2)
        def _(p):
            to0 = meta_ref[(OWN_RES + 2 * p) * LANES + ROWS + i] * LANES
            to1 = meta_ref[(OWN_RES + 2 * p + 1) * LANES + ROWS + i] * LANES
            total = jnp.zeros((size, 2 * size), jnp.float32)
            for s in range(0, slots, 2):
                left = jnp.concatenate(
                    [table[i * slots + s], table[i * slots + s + 1]], axis=1
                )
                base = [
                    meta_ref[(OWN_COLS + s + e) * LANES + ROWS + i] for e in range(2)
                ]
                total = total + jnp.dot(
                    left,
                    right(base[0], base[1], to0, to1),
                    preferred_element_type=jnp.float32,
                )
            square[p] = total
            rounded[p] = total.astype(jnp.bfloat16)

        @pl.loop(0, kept // 2)
        def _(p):
            to0 = meta_ref[(OWN_RES + 2 * p) * LANES + ROWS + i] * LANES
            to1 = meta_ref[(OWN_RES + 2 * p + 1) * LANES + ROWS + i] * LANES
            total = jnp.zeros((size, 2 * size), jnp.float32)
            for q in range(0, kept, 2):
                base = [
                    2 * W * LANES
                    - (LANES - 1) * meta_ref[(OWN_RES + q + e) * LANES + ROWS + i]
                    for e in range(2)
                ]
                total = total + jnp.dot(
                    rounded[q // 2],
                    right(base[0], base[1], to0, to1),
                    preferred_element_type=jnp.float32,
                )
            value = 3.0 * square[p] - 2.0 * total
            v0, v1 = value[:, :size], value[:, size:]
            lower = jnp.where(low, v0, pltpu.roll(v1, size // 2, 1))
            upper = jnp.where(low, pltpu.roll(v0, size // 2, 1), v1)
            out_ref[i, p] = jnp.where(even, lower, upper).astype(jnp.bfloat16)
            outgoing[r, p] = jnp.where(even, upper, lower).astype(jnp.bfloat16)

        @pl.when(r > 0)
        def _():
            send_row(r - 1).start()

    send_row(rows_here - 1).start()

    @pl.loop(0, rows_here)
    def _(r):
        send_row(r).wait()


def unpack_kernel(packed_ref, out_ref):
    pairs, size = packed_ref.shape[1], packed_ref.shape[2]
    for p in range(pairs):
        value = packed_ref[0, p]
        out_ref[0, 2 * p] = value[:, : size // 2]
        out_ref[0, 2 * p + 1] = value[:, size // 2 :]


def step(cap, chunks, ident, slots, kept, size):
    span = ROWS * slots
    return pl.pallas_call(
        functools.partial(step_kernel, cap, chunks, slots, kept),
        out_shape=jax.ShapeDtypeStruct((ROWS, kept // 2, size, size), jnp.bfloat16),
        in_specs=[pl.BlockSpec(memory_space=pltpu.SMEM)]
        + [pl.BlockSpec(memory_space=pl.ANY)] * 3,
        out_specs=pl.BlockSpec(memory_space=pltpu.VMEM),
        scratch_shapes=[
            pltpu.VMEM((3 * span + 1, size, size), jnp.bfloat16),
            pltpu.VMEM((kept // 2, size, 2 * size), jnp.float32),
            pltpu.VMEM((kept // 2, size, 2 * size), jnp.bfloat16),
            pltpu.VMEM((ROWS // 2, kept // 2, size, size), jnp.bfloat16),
            pltpu.SemaphoreType.DMA((3,)),
            pltpu.SemaphoreType.DMA((2 * chunks,)),
            pltpu.SemaphoreType.DMA((2 * chunks,)),
            pltpu.SemaphoreType.DMA((2 * chunks,)),
            pltpu.SemaphoreType.DMA((2 * chunks,)),
            pltpu.SemaphoreType.DMA((ROWS // 2,)),
            pltpu.SemaphoreType.DMA((ROWS // 2,)),
        ],
        compiler_params=pltpu.CompilerParams(
            collective_id=ident,
            has_side_effects=True,
            vmem_limit_bytes=40 * 2**20,
        ),
        name="step_%d" % cap,
    )


CAPS = (56, 64, 72, 80, 96)


def local(blocks, cols, res):
    rows, slots, edge, size = blocks.shape
    kept = res.shape[1]
    span = rows * slots
    meta = pl.pallas_call(
        index_kernel,
        out_shape=jax.ShapeDtypeStruct((META_ROWS, LANES), jnp.int32),
        name="index",
    )(cols.T, res.T)
    flat = meta.reshape(-1)
    own = blocks.reshape(span, edge, size)
    up, down = pl.pallas_call(
        functools.partial(pack_kernel, slots),
        out_shape=[jax.ShapeDtypeStruct((span + 1, edge, size), blocks.dtype)] * 2,
        in_specs=[
            pl.BlockSpec(memory_space=pltpu.SMEM),
            pl.BlockSpec(memory_space=pltpu.VMEM),
        ],
        name="pack",
    )(flat, own)
    most = meta[COUNT, 0]
    which = sum((most > cap).astype(jnp.int32) for cap in CAPS[:-1])
    packed = lax.switch(
        which,
        [step(cap, 4, n, slots, kept, size) for n, cap in enumerate(CAPS)],
        flat,
        own,
        up,
        down,
    )
    return pl.pallas_call(
        unpack_kernel,
        out_shape=jax.ShapeDtypeStruct((rows, kept, size, size // 2), blocks.dtype),
        grid=(rows,),
        in_specs=[pl.BlockSpec((1, kept // 2, size, size), lambda i: (i, 0, 0, 0))],
        out_specs=pl.BlockSpec((1, kept, size, size // 2), lambda i: (i, 0, 0, 0)),
        name="unpack",
    )(packed)


def solution(mesh):
    return jax.shard_map(
        local,
        mesh=mesh,
        in_specs=(P(("row", "col"), None, "depth", None), P(), P()),
        out_specs=P(("row", "col"), None, None, "depth"),
        check_vma=False,
    )
```

```python
import functools

import jax
import jax.numpy as jnp
from jax import lax
from jax.experimental import pallas as pl
from jax.experimental.pallas import tpu as pltpu
from jax.sharding import PartitionSpec as P

W = 8
ROWS = 8
LANES = 128
WIDE = 4
MESH = pl.DeviceIdType.MESH
OWN_COLS, OWN_RES, UP_SLOT, DOWN_SLOT, COUNT, META_ROWS = 40, 56, 72, 88, 104, 112


def group_index():
    return lax.axis_index("row") * lax.axis_size("col") + lax.axis_index("col")


def index_kernel(cols_ref, res_ref, meta_ref):
    slots, count = cols_ref.shape
    slots_kept = res_ref.shape[0]
    cols = cols_ref[...]
    res = res_ref[...]
    row = lax.broadcasted_iota(jnp.int32, (slots, count), 1)
    half = count // 2

    def offset(values):
        t = values - row
        t = jnp.where(t > half, t - count, t)
        return jnp.where(t < -half, t + count, t)

    present = cols >= 0
    off = offset(cols)
    in_group = row & (ROWS - 1)
    lane_group = in_group[:1]
    away = 4 * W
    off = jnp.where(present, off, away)
    extra = jnp.full((16 - slots, count), away, jnp.int32)
    off_all = jnp.concatenate([off, extra], axis=0)
    kept_all = jnp.concatenate([offset(res), extra], axis=0)

    def needed(sign):
        need = jnp.zeros((slots, count), jnp.int32)
        for d in range(1, W + 1):
            step = sign * d
            turn = count - d if sign > 0 else d
            kept_there = pltpu.roll(kept_all, turn, 1)
            off_there = pltpu.roll(off_all, turn, 1)
            reads = (kept_there == -step) | (off_there == -step)
            reads = jnp.max(jnp.where(reads, 1, 0), axis=0, keepdims=True)
            if sign > 0:
                inside = lane_group + d >= ROWS
            else:
                inside = lane_group - d < 0
            reads = jnp.where(inside, reads, 0)
            hit = jnp.zeros((slots, count), jnp.int32)
            for q in range(slots_kept):
                hit = jnp.where(off - step == kept_there[q : q + 1], 1, hit)
            need = jnp.maximum(need, hit * reads)
        return present & (need > 0)

    need_up = needed(1)
    need_down = needed(-1)

    def positions(need):
        ones = jnp.where(need, 1, 0)
        run = jnp.zeros((1, count), jnp.int32)
        within = []
        for s in range(slots):
            within.append(run)
            run = run + ones[s : s + 1]
        before = jnp.zeros((1, count), jnp.int32)
        wide = jnp.broadcast_to(run, (8, count))
        for j in range(1, ROWS):
            before = before + jnp.where(lane_group >= j, pltpu.roll(wide, j, 1)[:1], 0)
        return jnp.concatenate([w + before for w in within], axis=0), before + run

    pos_up, total_up = positions(need_up)
    pos_down, total_down = positions(need_down)
    most = jnp.max(jnp.maximum(total_up, total_down))
    which = jnp.int32(0)
    for cap in CAPS[:-1]:
        which = which + jnp.where(most > cap, 1, 0)

    first = group_index() * ROWS
    shift = lax.rem(count - first + ROWS, count)

    def window(values):
        padded = jnp.concatenate(
            [values, jnp.zeros((16 - slots, count), jnp.int32)], axis=0
        )
        return pltpu.roll(padded, shift, 1)[:, :LANES]

    span = ROWS * slots
    empty = 3 * span
    lane = lax.broadcasted_iota(jnp.int32, (16, LANES), 1)
    slot = lax.broadcasted_iota(jnp.int32, (16, LANES), 0)
    up_slot = window(jnp.where(need_up, pos_up, span))
    down_slot = window(jnp.where(need_down, pos_down, span))
    off_w = window(off)
    here = off_w < 4 * W
    place = jnp.where(
        lane < ROWS,
        jnp.where(up_slot < span, span + up_slot, empty),
        jnp.where(
            lane < 2 * ROWS,
            (lane - ROWS) * slots + slot,
            jnp.where(down_slot < span, 2 * span + down_slot, empty),
        ),
    )
    place = jnp.where(here & (lane < 3 * ROWS), place, empty)
    wanted = lax.broadcasted_iota(jnp.int32, (OWN_COLS, LANES), 0) - 2 * W
    dense = jnp.full((OWN_COLS, LANES), empty, jnp.int32)
    for s in range(slots):
        dense = jnp.where(off_w[s : s + 1] == wanted, place[s : s + 1], dense)
    meta_ref[:OWN_COLS] = dense
    reach_col = off_w + lane
    meta_ref[OWN_COLS:OWN_RES] = jnp.where(
        here, (2 * W - reach_col) * LANES + reach_col, LANES - 1
    )
    meta_ref[OWN_RES:UP_SLOT] = window(offset(res)) + lane
    meta_ref[UP_SLOT:DOWN_SLOT] = up_slot
    meta_ref[DOWN_SLOT:COUNT] = down_slot
    meta_ref[COUNT:] = jnp.full((META_ROWS - COUNT, LANES), which, jnp.int32)


def pack_kernel(slots, meta_ref, blocks_ref, up_ref, down_ref):
    @pl.loop(0, slots)
    def _(s):
        for u in range(ROWS):
            block = blocks_ref[u * slots + s]
            up_ref[meta_ref[(UP_SLOT + s) * LANES + ROWS + u]] = block
            down_ref[meta_ref[(DOWN_SLOT + s) * LANES + ROWS + u]] = block


def step_kernel(
    cap,
    chunks,
    slots,
    kept,
    meta_ref,
    blocks_ref,
    up_ref,
    down_ref,
    out_ref,
    table,
    square,
    rounded,
    outgoing,
    own_sem,
    send_sem,
    recv_sem,
    pass_send_sem,
    pass_recv_sem,
    out_send_sem,
    out_recv_sem,
):
    row, col, depth = (lax.axis_index(a) for a in ("row", "col", "depth"))
    row_count, col_count = lax.axis_size("row"), lax.axis_size("col")
    groups = row_count * col_count
    group = row * col_count + col
    following = lax.rem(group + 1, groups)
    preceding = lax.rem(group + groups - 1, groups)
    sibling = (row, col, 1 - depth)
    after = (following // col_count, lax.rem(following, col_count), depth)
    before = (preceding // col_count, lax.rem(preceding, col_count), depth)

    barrier = pltpu.get_barrier_semaphore()
    for device in (sibling, after, before):
        pl.semaphore_signal(barrier, inc=1, device_id=device, device_id_type=MESH)
    pl.semaphore_wait(barrier, 3)

    span = ROWS * slots
    part = cap // chunks
    edge = blocks_ref.shape[1]
    mine = pl.ds(pl.multiple_of(depth * edge, edge), edge)

    halo = []
    for c in range(chunks):
        for way, (source, device) in enumerate(((up_ref, after), (down_ref, before))):
            start = span * (way + 1) + c * part
            k = 2 * c + way
            copy = pltpu.make_async_remote_copy(
                src_ref=source.at[pl.ds(c * part, part)],
                dst_ref=table.at[pl.ds(start, part), mine, :],
                send_sem=send_sem.at[k],
                recv_sem=recv_sem.at[k],
                device_id=device,
                device_id_type=MESH,
            )
            copy.start()
            halo.append((k, start, copy))
    keep = pltpu.make_async_copy(
        blocks_ref, table.at[pl.ds(0, span), mine, :], own_sem.at[0]
    )
    keep.start()
    share = pltpu.make_async_remote_copy(
        src_ref=blocks_ref,
        dst_ref=table.at[pl.ds(0, span), mine, :],
        send_sem=own_sem.at[1],
        recv_sem=own_sem.at[2],
        device_id=sibling,
        device_id_type=MESH,
    )
    share.start()
    table[3 * span] = jnp.zeros(table.shape[1:], table.dtype)
    passed = []
    for k, start, copy in halo:
        copy.wait_recv()
        forward = pltpu.make_async_remote_copy(
            src_ref=table.at[pl.ds(start, part), mine, :],
            dst_ref=table.at[pl.ds(start, part), mine, :],
            send_sem=pass_send_sem.at[k],
            recv_sem=pass_recv_sem.at[k],
            device_id=sibling,
            device_id_type=MESH,
        )
        forward.start()
        passed.append(forward)
    keep.wait()
    share.wait()
    for forward in passed:
        forward.wait()
    for _, _, copy in halo:
        copy.wait_send()

    rows_here = ROWS // 2
    size = table.shape[2]
    even = depth == 0
    half = size // 2

    def right(bases, to):
        return jnp.concatenate(
            [
                jnp.concatenate([table[meta_ref[b + t]] for t in to], axis=1)
                for b in bases
            ],
            axis=0,
        )

    def send_row(r):
        return pltpu.make_async_remote_copy(
            src_ref=outgoing.at[r],
            dst_ref=out_ref.at[depth * rows_here + r],
            send_sem=out_send_sem.at[r],
            recv_sem=out_recv_sem.at[r],
            device_id=sibling,
            device_id_type=MESH,
        )

    @pl.loop(0, rows_here)
    def _(r):
        i = depth * rows_here + r

        def targets(p):
            return [
                meta_ref[(OWN_RES + WIDE * p + e) * LANES + ROWS + i] * LANES
                for e in range(WIDE)
            ]

        @pl.loop(0, kept // WIDE)
        def _(p):
            to = targets(p)
            total = jnp.zeros((size, WIDE * size), jnp.float32)
            for s in range(0, slots, 2):
                left = jnp.concatenate(
                    [table[i * slots + s], table[i * slots + s + 1]], axis=1
                )
                bases = [
                    meta_ref[(OWN_COLS + s + e) * LANES + ROWS + i] for e in range(2)
                ]
                total = total + jnp.dot(
                    left, right(bases, to), preferred_element_type=jnp.float32
                )
            square[p] = total
            rounded[p] = total.astype(jnp.bfloat16)

        @pl.loop(0, kept // WIDE)
        def _(p):
            to = targets(p)
            total = jnp.zeros((size, WIDE * size), jnp.float32)
            for q in range(0, kept, 2):
                bases = [
                    2 * W * LANES
                    - (LANES - 1) * meta_ref[(OWN_RES + q + e) * LANES + ROWS + i]
                    for e in range(2)
                ]
                at = q % WIDE * size
                total = total + jnp.dot(
                    rounded[q // WIDE, :, at : at + 2 * size],
                    right(bases, to),
                    preferred_element_type=jnp.float32,
                )
            value = (3.0 * square[p] - 2.0 * total).astype(jnp.bfloat16)
            for e in range(WIDE):
                turned = value[:, e * size : (e + 1) * size].T
                top, bottom = turned[:half], turned[half:]
                out_ref[i, WIDE * p + e] = jnp.where(even, top, bottom)
                outgoing[r, WIDE * p + e] = jnp.where(even, bottom, top)

        @pl.when(r > 0)
        def _():
            send_row(r - 1).start()

    send_row(rows_here - 1).start()

    @pl.loop(0, rows_here)
    def _(r):
        send_row(r).wait()


def step(cap, chunks, ident, slots, kept, size):
    span = ROWS * slots
    return pl.pallas_call(
        functools.partial(step_kernel, cap, chunks, slots, kept),
        out_shape=jax.ShapeDtypeStruct((ROWS, kept, size // 2, size), jnp.bfloat16),
        in_specs=[pl.BlockSpec(memory_space=pltpu.SMEM)]
        + [pl.BlockSpec(memory_space=pl.ANY)] * 3,
        out_specs=pl.BlockSpec(memory_space=pltpu.VMEM),
        scratch_shapes=[
            pltpu.VMEM((3 * span + 1, size, size), jnp.bfloat16),
            pltpu.VMEM((kept // WIDE, size, WIDE * size), jnp.float32),
            pltpu.VMEM((kept // WIDE, size, WIDE * size), jnp.bfloat16),
            pltpu.VMEM((ROWS // 2, kept, size // 2, size), jnp.bfloat16),
            pltpu.SemaphoreType.DMA((3,)),
            pltpu.SemaphoreType.DMA((2 * chunks,)),
            pltpu.SemaphoreType.DMA((2 * chunks,)),
            pltpu.SemaphoreType.DMA((2 * chunks,)),
            pltpu.SemaphoreType.DMA((2 * chunks,)),
            pltpu.SemaphoreType.DMA((ROWS // 2,)),
            pltpu.SemaphoreType.DMA((ROWS // 2,)),
        ],
        compiler_params=pltpu.CompilerParams(
            collective_id=ident,
            has_side_effects=True,
            vmem_limit_bytes=40 * 2**20,
        ),
        name="step_%d" % cap,
    )


CAPS = (52, 56, 60, 64, 72, 96)


def local(blocks, cols, res):
    rows, slots, edge, size = blocks.shape
    kept = res.shape[1]
    span = rows * slots
    meta = pl.pallas_call(
        index_kernel,
        out_shape=jax.ShapeDtypeStruct((META_ROWS, LANES), jnp.int32),
        name="index",
    )(cols.T, res.T)
    flat = meta.reshape(-1)
    own = blocks.reshape(span, edge, size)
    up, down = pl.pallas_call(
        functools.partial(pack_kernel, slots),
        out_shape=[jax.ShapeDtypeStruct((span + 1, edge, size), blocks.dtype)] * 2,
        in_specs=[
            pl.BlockSpec(memory_space=pltpu.SMEM),
            pl.BlockSpec(memory_space=pltpu.VMEM),
        ],
        name="pack",
    )(flat, own)
    which = meta[COUNT, 0]
    packed = lax.switch(
        which,
        [step(cap, 4, n, slots, kept, size) for n, cap in enumerate(CAPS)],
        flat,
        own,
        up,
        down,
    )
    return jnp.swapaxes(packed, 2, 3)


def solution(mesh):
    return jax.shard_map(
        local,
        mesh=mesh,
        in_specs=(P(("row", "col"), None, "depth", None), P(), P()),
        out_specs=P(("row", "col"), None, None, "depth"),
        check_vma=False,
    )
```

```python
import functools

import jax
import jax.numpy as jnp
from jax import lax
from jax.experimental import pallas as pl
from jax.experimental.pallas import tpu as pltpu
from jax.sharding import PartitionSpec as P

W = 8
ROWS = 8
LANES = 128
WIDE = 4
MESH = pl.DeviceIdType.MESH
OWN_COLS, OWN_RES, UP_SLOT, DOWN_SLOT, COUNT, META_ROWS = 40, 56, 72, 88, 104, 112


def group_index():
    return lax.axis_index("row") * lax.axis_size("col") + lax.axis_index("col")


def index_kernel(cols_ref, res_ref, meta_ref):
    slots, count = cols_ref.shape
    slots_kept = res_ref.shape[0]
    cols = cols_ref[...]
    res = res_ref[...]
    row = lax.broadcasted_iota(jnp.int32, (slots, count), 1)
    half = count // 2

    def offset(values):
        t = values - row
        t = jnp.where(t > half, t - count, t)
        return jnp.where(t < -half, t + count, t)

    present = cols >= 0
    off = offset(cols)
    in_group = row & (ROWS - 1)
    lane_group = in_group[:1]
    away = 4 * W
    off = jnp.where(present, off, away)
    extra = jnp.full((16 - slots, count), away, jnp.int32)
    off_all = jnp.concatenate([off, extra], axis=0)
    kept_all = jnp.concatenate([offset(res), extra], axis=0)

    def needed(sign):
        need = jnp.zeros((slots, count), jnp.int32)
        for d in range(1, W + 1):
            step = sign * d
            turn = count - d if sign > 0 else d
            kept_there = pltpu.roll(kept_all, turn, 1)
            off_there = pltpu.roll(off_all, turn, 1)
            reads = (kept_there == -step) | (off_there == -step)
            reads = jnp.max(jnp.where(reads, 1, 0), axis=0, keepdims=True)
            if sign > 0:
                inside = lane_group + d >= ROWS
            else:
                inside = lane_group - d < 0
            reads = jnp.where(inside, reads, 0)
            hit = jnp.zeros((slots, count), jnp.int32)
            for q in range(slots_kept):
                hit = jnp.where(off - step == kept_there[q : q + 1], 1, hit)
            need = jnp.maximum(need, hit * reads)
        return present & (need > 0)

    need_up = needed(1)
    need_down = needed(-1)

    def positions(need):
        ones = jnp.where(need, 1, 0)
        run = jnp.zeros((1, count), jnp.int32)
        within = []
        for s in range(slots):
            within.append(run)
            run = run + ones[s : s + 1]
        before = jnp.zeros((1, count), jnp.int32)
        wide = jnp.broadcast_to(run, (8, count))
        for j in range(1, ROWS):
            before = before + jnp.where(lane_group >= j, pltpu.roll(wide, j, 1)[:1], 0)
        return jnp.concatenate([w + before for w in within], axis=0), before + run

    pos_up, total_up = positions(need_up)
    pos_down, total_down = positions(need_down)
    most = jnp.max(jnp.maximum(total_up, total_down))
    which = jnp.int32(0)
    for cap in CAPS[:-1]:
        which = which + jnp.where(most > cap, 1, 0)

    first = group_index() * ROWS
    shift = lax.rem(count - first + ROWS, count)

    def window(values):
        padded = jnp.concatenate(
            [values, jnp.zeros((16 - slots, count), jnp.int32)], axis=0
        )
        return pltpu.roll(padded, shift, 1)[:, :LANES]

    span = ROWS * slots
    empty = 3 * span
    lane = lax.broadcasted_iota(jnp.int32, (16, LANES), 1)
    slot = lax.broadcasted_iota(jnp.int32, (16, LANES), 0)
    up_slot = window(jnp.where(need_up, pos_up, span))
    down_slot = window(jnp.where(need_down, pos_down, span))
    off_w = window(off)
    here = off_w < 4 * W
    place = jnp.where(
        lane < ROWS,
        jnp.where(up_slot < span, span + up_slot, empty),
        jnp.where(
            lane < 2 * ROWS,
            (lane - ROWS) * slots + slot,
            jnp.where(down_slot < span, 2 * span + down_slot, empty),
        ),
    )
    place = jnp.where(here & (lane < 3 * ROWS), place, empty)
    wanted = lax.broadcasted_iota(jnp.int32, (OWN_COLS, LANES), 0) - 2 * W
    dense = jnp.full((OWN_COLS, LANES), empty, jnp.int32)
    for s in range(slots):
        dense = jnp.where(off_w[s : s + 1] == wanted, place[s : s + 1], dense)
    meta_ref[:OWN_COLS] = dense
    reach_col = off_w + lane
    meta_ref[OWN_COLS:OWN_RES] = jnp.where(
        here, (2 * W - reach_col) * LANES + reach_col, LANES - 1
    )
    meta_ref[OWN_RES:UP_SLOT] = window(offset(res)) + lane
    meta_ref[UP_SLOT:DOWN_SLOT] = up_slot
    meta_ref[DOWN_SLOT:COUNT] = down_slot
    meta_ref[COUNT:] = jnp.full((META_ROWS - COUNT, LANES), which, jnp.int32)


def pack_kernel(slots, meta_ref, blocks_ref, up_ref, down_ref):
    @pl.loop(0, slots)
    def _(s):
        for u in range(ROWS):
            block = blocks_ref[u * slots + s]
            up_ref[meta_ref[(UP_SLOT + s) * LANES + ROWS + u]] = block
            down_ref[meta_ref[(DOWN_SLOT + s) * LANES + ROWS + u]] = block


def step_kernel(
    cap,
    slots,
    kept,
    meta_ref,
    blocks_ref,
    up_ref,
    down_ref,
    out_ref,
    table,
    square,
    rounded,
    outgoing,
    own_sem,
    send_sem,
    recv_sem,
    pass_send_sem,
    pass_recv_sem,
    out_send_sem,
    out_recv_sem,
):
    row, col, depth = (lax.axis_index(a) for a in ("row", "col", "depth"))
    row_count, col_count = lax.axis_size("row"), lax.axis_size("col")
    groups = row_count * col_count
    group = row * col_count + col
    following = lax.rem(group + 1, groups)
    preceding = lax.rem(group + groups - 1, groups)
    sibling = (row, col, 1 - depth)
    after = (following // col_count, lax.rem(following, col_count), depth)
    before = (preceding // col_count, lax.rem(preceding, col_count), depth)

    barrier = pltpu.get_barrier_semaphore()
    for device in (sibling, after, before):
        pl.semaphore_signal(barrier, inc=1, device_id=device, device_id_type=MESH)
    pl.semaphore_wait(barrier, 3)

    span = ROWS * slots
    edge = blocks_ref.shape[1]
    mine = pl.ds(pl.multiple_of(depth * edge, edge), edge)

    halo = []
    done = 0
    for c, part in enumerate(pieces(cap)):
        for way, (source, device) in enumerate(((up_ref, after), (down_ref, before))):
            start = span * (way + 1) + done
            k = 2 * c + way
            copy = pltpu.make_async_remote_copy(
                src_ref=source.at[pl.ds(done, part)],
                dst_ref=table.at[pl.ds(start, part), mine, :],
                send_sem=send_sem.at[k],
                recv_sem=recv_sem.at[k],
                device_id=device,
                device_id_type=MESH,
            )
            copy.start()
            halo.append((k, start, part, copy))
        done += part
    keep = pltpu.make_async_copy(
        blocks_ref, table.at[pl.ds(0, span), mine, :], own_sem.at[0]
    )
    keep.start()
    share = pltpu.make_async_remote_copy(
        src_ref=blocks_ref,
        dst_ref=table.at[pl.ds(0, span), mine, :],
        send_sem=own_sem.at[1],
        recv_sem=own_sem.at[2],
        device_id=sibling,
        device_id_type=MESH,
    )
    share.start()
    table[3 * span] = jnp.zeros(table.shape[1:], table.dtype)
    passed = []
    for k, start, part, copy in halo:
        copy.wait_recv()
        forward = pltpu.make_async_remote_copy(
            src_ref=table.at[pl.ds(start, part), mine, :],
            dst_ref=table.at[pl.ds(start, part), mine, :],
            send_sem=pass_send_sem.at[k],
            recv_sem=pass_recv_sem.at[k],
            device_id=sibling,
            device_id_type=MESH,
        )
        forward.start()
        passed.append(forward)
    keep.wait()
    share.wait()
    for forward in passed:
        forward.wait()
    for _, _, _, copy in halo:
        copy.wait_send()

    rows_here = ROWS // 2
    size = table.shape[2]
    even = depth == 0
    half = size // 2

    def right(bases, to):
        return jnp.concatenate(
            [
                jnp.concatenate([table[meta_ref[b + t]] for t in to], axis=1)
                for b in bases
            ],
            axis=0,
        )

    steps = kept // WIDE

    def send(n):
        at = n % steps * WIDE
        return pltpu.make_async_remote_copy(
            src_ref=outgoing.at[n],
            dst_ref=out_ref.at[depth * rows_here + n // steps, pl.ds(at, WIDE)],
            send_sem=out_send_sem.at[n],
            recv_sem=out_recv_sem.at[n],
            device_id=sibling,
            device_id_type=MESH,
        )

    @pl.loop(0, rows_here)
    def _(r):
        i = depth * rows_here + r

        def targets(p):
            return [
                meta_ref[(OWN_RES + WIDE * p + e) * LANES + ROWS + i] * LANES
                for e in range(WIDE)
            ]

        @pl.loop(0, kept // WIDE)
        def _(p):
            to = targets(p)
            total = jnp.zeros((size, WIDE * size), jnp.float32)
            for s in range(0, slots, 2):
                left = jnp.concatenate(
                    [table[i * slots + s], table[i * slots + s + 1]], axis=1
                )
                bases = [
                    meta_ref[(OWN_COLS + s + e) * LANES + ROWS + i] for e in range(2)
                ]
                total = total + jnp.dot(
                    left, right(bases, to), preferred_element_type=jnp.float32
                )
            square[p] = total
            rounded[p] = total.astype(jnp.bfloat16)

        @pl.loop(0, kept // WIDE)
        def _(p):
            to = targets(p)
            total = jnp.zeros((size, WIDE * size), jnp.float32)
            for q in range(0, kept, 2):
                bases = [
                    2 * W * LANES
                    - (LANES - 1) * meta_ref[(OWN_RES + q + e) * LANES + ROWS + i]
                    for e in range(2)
                ]
                at = q % WIDE * size
                total = total + jnp.dot(
                    rounded[q // WIDE, :, at : at + 2 * size],
                    right(bases, to),
                    preferred_element_type=jnp.float32,
                )
            value = (3.0 * square[p] - 2.0 * total).astype(jnp.bfloat16)
            n = r * steps + p
            for e in range(WIDE):
                turned = value[:, e * size : (e + 1) * size].T
                top, bottom = turned[:half], turned[half:]
                out_ref[i, WIDE * p + e] = jnp.where(even, top, bottom)
                outgoing[n, e] = jnp.where(even, bottom, top)

            @pl.when(n > 0)
            def _():
                send(n - 1).start()

    send(rows_here * steps - 1).start()

    @pl.loop(0, rows_here * steps)
    def _(n):
        send(n).wait()


def step(cap, ident, slots, kept, size):
    span = ROWS * slots
    chunks = len(pieces(cap))
    sends = ROWS // 2 * (kept // WIDE)
    return pl.pallas_call(
        functools.partial(step_kernel, cap, slots, kept),
        out_shape=jax.ShapeDtypeStruct((ROWS, kept, size // 2, size), jnp.bfloat16),
        in_specs=[pl.BlockSpec(memory_space=pltpu.SMEM)]
        + [pl.BlockSpec(memory_space=pl.ANY)] * 3,
        out_specs=pl.BlockSpec(memory_space=pltpu.VMEM),
        scratch_shapes=[
            pltpu.VMEM((3 * span + 1, size, size), jnp.bfloat16),
            pltpu.VMEM((kept // WIDE, size, WIDE * size), jnp.float32),
            pltpu.VMEM((kept // WIDE, size, WIDE * size), jnp.bfloat16),
            pltpu.VMEM((sends, WIDE, size // 2, size), jnp.bfloat16),
            pltpu.SemaphoreType.DMA((3,)),
            pltpu.SemaphoreType.DMA((2 * chunks,)),
            pltpu.SemaphoreType.DMA((2 * chunks,)),
            pltpu.SemaphoreType.DMA((2 * chunks,)),
            pltpu.SemaphoreType.DMA((2 * chunks,)),
            pltpu.SemaphoreType.DMA((sends,)),
            pltpu.SemaphoreType.DMA((sends,)),
        ],
        compiler_params=pltpu.CompilerParams(
            collective_id=ident,
            has_side_effects=True,
            vmem_limit_bytes=40 * 2**20,
        ),
        name="step_%d" % cap,
    )


CAPS = (54, 56, 58, 60, 62, 64, 72, 96)


def pieces(cap):
    head, tail = cap - 16, [8, 4, 4]
    return [head % 16] * (head % 16 > 0) + [16] * (head // 16) + tail


def local(blocks, cols, res):
    rows, slots, edge, size = blocks.shape
    kept = res.shape[1]
    span = rows * slots
    meta = pl.pallas_call(
        index_kernel,
        out_shape=jax.ShapeDtypeStruct((META_ROWS, LANES), jnp.int32),
        name="index",
    )(cols.T, res.T)
    flat = meta.reshape(-1)
    own = blocks.reshape(span, edge, size)
    up, down = pl.pallas_call(
        functools.partial(pack_kernel, slots),
        out_shape=[jax.ShapeDtypeStruct((span + 1, edge, size), blocks.dtype)] * 2,
        in_specs=[
            pl.BlockSpec(memory_space=pltpu.SMEM),
            pl.BlockSpec(memory_space=pltpu.VMEM),
        ],
        name="pack",
    )(flat, own)
    which = meta[COUNT, 0]
    packed = lax.switch(
        which,
        [step(cap, n, slots, kept, size) for n, cap in enumerate(CAPS)],
        flat,
        own,
        up,
        down,
    )
    return jnp.swapaxes(packed, 2, 3)


def solution(mesh):
    return jax.shard_map(
        local,
        mesh=mesh,
        in_specs=(P(("row", "col"), None, "depth", None), P(), P()),
        out_specs=P(("row", "col"), None, None, "depth"),
        check_vma=False,
    )
```

```python
import functools

import jax
import jax.numpy as jnp
from jax import lax
from jax.experimental import pallas as pl
from jax.experimental.pallas import tpu as pltpu
from jax.sharding import PartitionSpec as P

W = 8
ROWS = 8
LANES = 128
WIDE = 4
MESH = pl.DeviceIdType.MESH
OWN_COLS, OWN_RES, UP_SLOT, DOWN_SLOT, COUNT, META_ROWS = 40, 56, 72, 88, 104, 112


def group_index():
    return lax.axis_index("row") * lax.axis_size("col") + lax.axis_index("col")


def index_kernel(cols_ref, res_ref, meta_ref):
    slots, count = cols_ref.shape
    slots_kept = res_ref.shape[0]
    cols = cols_ref[...]
    res = res_ref[...]
    row = lax.broadcasted_iota(jnp.int32, (slots, count), 1)
    half = count // 2

    def offset(values):
        t = values - row
        t = jnp.where(t > half, t - count, t)
        return jnp.where(t < -half, t + count, t)

    present = cols >= 0
    off = offset(cols)
    in_group = row & (ROWS - 1)
    lane_group = in_group[:1]
    away = 4 * W
    off = jnp.where(present, off, away)
    extra = jnp.full((16 - slots, count), away, jnp.int32)
    off_all = jnp.concatenate([off, extra], axis=0)
    kept_all = jnp.concatenate([offset(res), extra], axis=0)

    def needed(sign):
        need = jnp.zeros((slots, count), jnp.int32)
        for d in range(1, W + 1):
            step = sign * d
            turn = count - d if sign > 0 else d
            kept_there = pltpu.roll(kept_all, turn, 1)
            off_there = pltpu.roll(off_all, turn, 1)
            reads = (kept_there == -step) | (off_there == -step)
            reads = jnp.max(jnp.where(reads, 1, 0), axis=0, keepdims=True)
            if sign > 0:
                inside = lane_group + d >= ROWS
            else:
                inside = lane_group - d < 0
            reads = jnp.where(inside, reads, 0)
            hit = jnp.zeros((slots, count), jnp.int32)
            for q in range(slots_kept):
                hit = jnp.where(off - step == kept_there[q : q + 1], 1, hit)
            need = jnp.maximum(need, hit * reads)
        return present & (need > 0)

    need_up = needed(1)
    need_down = needed(-1)

    def positions(need):
        ones = jnp.where(need, 1, 0)
        run = jnp.zeros((1, count), jnp.int32)
        within = []
        for s in range(slots):
            within.append(run)
            run = run + ones[s : s + 1]
        before = jnp.zeros((1, count), jnp.int32)
        wide = jnp.broadcast_to(run, (8, count))
        for j in range(1, ROWS):
            before = before + jnp.where(lane_group >= j, pltpu.roll(wide, j, 1)[:1], 0)
        return jnp.concatenate([w + before for w in within], axis=0), before + run

    pos_up, total_up = positions(need_up)
    pos_down, total_down = positions(need_down)
    most = jnp.max(jnp.maximum(total_up, total_down))
    which = jnp.int32(0)
    for cap in CAPS[:-1]:
        which = which + jnp.where(most > cap, 1, 0)

    first = group_index() * ROWS
    shift = lax.rem(count - first + ROWS, count)

    def window(values):
        padded = jnp.concatenate(
            [values, jnp.zeros((16 - slots, count), jnp.int32)], axis=0
        )
        return pltpu.roll(padded, shift, 1)[:, :LANES]

    span = ROWS * slots
    empty = 3 * span
    lane = lax.broadcasted_iota(jnp.int32, (16, LANES), 1)
    slot = lax.broadcasted_iota(jnp.int32, (16, LANES), 0)
    up_slot = window(jnp.where(need_up, pos_up, span))
    down_slot = window(jnp.where(need_down, pos_down, span))
    off_w = window(off)
    here = off_w < 4 * W
    place = jnp.where(
        lane < ROWS,
        jnp.where(up_slot < span, span + up_slot, empty),
        jnp.where(
            lane < 2 * ROWS,
            (lane - ROWS) * slots + slot,
            jnp.where(down_slot < span, 2 * span + down_slot, empty),
        ),
    )
    place = jnp.where(here & (lane < 3 * ROWS), place, empty)
    wanted = lax.broadcasted_iota(jnp.int32, (OWN_COLS, LANES), 0) - 2 * W
    dense = jnp.full((OWN_COLS, LANES), empty, jnp.int32)
    for s in range(slots):
        dense = jnp.where(off_w[s : s + 1] == wanted, place[s : s + 1], dense)
    meta_ref[:OWN_COLS] = dense
    reach_col = off_w + lane
    meta_ref[OWN_COLS:OWN_RES] = jnp.where(
        here, (2 * W - reach_col) * LANES + reach_col, LANES - 1
    )
    meta_ref[OWN_RES:UP_SLOT] = window(offset(res)) + lane
    meta_ref[UP_SLOT:DOWN_SLOT] = up_slot
    meta_ref[DOWN_SLOT:COUNT] = down_slot
    meta_ref[COUNT:] = jnp.full((META_ROWS - COUNT, LANES), which, jnp.int32)


def pack_kernel(slots, meta_ref, blocks_ref, up_ref, down_ref):
    @pl.loop(0, slots)
    def _(s):
        for u in range(ROWS):
            block = blocks_ref[u * slots + s]
            up_ref[meta_ref[(UP_SLOT + s) * LANES + ROWS + u]] = block
            down_ref[meta_ref[(DOWN_SLOT + s) * LANES + ROWS + u]] = block


def step_kernel(
    cap,
    slots,
    kept,
    meta_ref,
    blocks_ref,
    up_ref,
    down_ref,
    out_ref,
    table,
    square,
    rounded,
    outgoing,
    own_sem,
    send_sem,
    recv_sem,
    pass_send_sem,
    pass_recv_sem,
    out_send_sem,
    out_recv_sem,
):
    row, col, depth = (lax.axis_index(a) for a in ("row", "col", "depth"))
    row_count, col_count = lax.axis_size("row"), lax.axis_size("col")
    groups = row_count * col_count
    group = row * col_count + col
    following = lax.rem(group + 1, groups)
    preceding = lax.rem(group + groups - 1, groups)
    sibling = (row, col, 1 - depth)
    after = (following // col_count, lax.rem(following, col_count), depth)
    before = (preceding // col_count, lax.rem(preceding, col_count), depth)

    barrier = pltpu.get_barrier_semaphore()
    for device in (sibling, after, before):
        pl.semaphore_signal(barrier, inc=1, device_id=device, device_id_type=MESH)
    pl.semaphore_wait(barrier, 3)

    span = ROWS * slots
    edge = blocks_ref.shape[1]
    mine = pl.ds(pl.multiple_of(depth * edge, edge), edge)

    halo = []
    done = 0
    for c, part in enumerate(pieces(cap)):
        for way, (source, device) in enumerate(((up_ref, after), (down_ref, before))):
            start = span * (way + 1) + done
            k = 2 * c + way
            copy = pltpu.make_async_remote_copy(
                src_ref=source.at[pl.ds(done, part)],
                dst_ref=table.at[pl.ds(start, part), mine, :],
                send_sem=send_sem.at[k],
                recv_sem=recv_sem.at[k],
                device_id=device,
                device_id_type=MESH,
            )
            copy.start()
            halo.append((k, start, part, copy))
        done += part
    keep = pltpu.make_async_copy(
        blocks_ref, table.at[pl.ds(0, span), mine, :], own_sem.at[0]
    )
    keep.start()
    share = pltpu.make_async_remote_copy(
        src_ref=blocks_ref,
        dst_ref=table.at[pl.ds(0, span), mine, :],
        send_sem=own_sem.at[1],
        recv_sem=own_sem.at[2],
        device_id=sibling,
        device_id_type=MESH,
    )
    share.start()
    table[3 * span] = jnp.zeros(table.shape[1:], table.dtype)
    passed = []
    for k, start, part, copy in halo:
        copy.wait_recv()
        forward = pltpu.make_async_remote_copy(
            src_ref=table.at[pl.ds(start, part), mine, :],
            dst_ref=table.at[pl.ds(start, part), mine, :],
            send_sem=pass_send_sem.at[k],
            recv_sem=pass_recv_sem.at[k],
            device_id=sibling,
            device_id_type=MESH,
        )
        forward.start()
        passed.append(forward)
    keep.wait()
    share.wait()
    for forward in passed:
        forward.wait()
    for _, _, _, copy in halo:
        copy.wait_send()

    rows_here = ROWS // 2
    size = table.shape[2]
    even = depth == 0
    half = size // 2

    def right(bases, to):
        return jnp.concatenate(
            [
                jnp.concatenate([table[meta_ref[b + t]] for t in to], axis=1)
                for b in bases
            ],
            axis=0,
        )

    def send_row(r):
        return pltpu.make_async_remote_copy(
            src_ref=outgoing.at[r],
            dst_ref=out_ref.at[depth * rows_here + r],
            send_sem=out_send_sem.at[r],
            recv_sem=out_recv_sem.at[r],
            device_id=sibling,
            device_id_type=MESH,
        )

    @pl.loop(0, rows_here)
    def _(r):
        i = depth * rows_here + r

        def targets(p):
            return [
                meta_ref[(OWN_RES + WIDE * p + e) * LANES + ROWS + i] * LANES
                for e in range(WIDE)
            ]

        @pl.loop(0, kept // WIDE)
        def _(p):
            to = targets(p)
            total = jnp.zeros((size, WIDE * size), jnp.float32)
            for s in range(0, slots, 2):
                left = jnp.concatenate(
                    [table[i * slots + s], table[i * slots + s + 1]], axis=1
                )
                bases = [
                    meta_ref[(OWN_COLS + s + e) * LANES + ROWS + i] for e in range(2)
                ]
                total = total + jnp.dot(
                    left, right(bases, to), preferred_element_type=jnp.float32
                )
            square[p] = total
            rounded[p] = total.astype(jnp.bfloat16)

        @pl.loop(0, kept // WIDE)
        def _(p):
            to = targets(p)
            total = jnp.zeros((size, WIDE * size), jnp.float32)
            for q in range(0, kept, 2):
                bases = [
                    2 * W * LANES
                    - (LANES - 1) * meta_ref[(OWN_RES + q + e) * LANES + ROWS + i]
                    for e in range(2)
                ]
                at = q % WIDE * size
                total = total + jnp.dot(
                    rounded[q // WIDE, :, at : at + 2 * size],
                    right(bases, to),
                    preferred_element_type=jnp.float32,
                )
            value = (3.0 * square[p] - 2.0 * total).astype(jnp.bfloat16)
            for e in range(WIDE):
                turned = value[:, e * size : (e + 1) * size].T
                top, bottom = turned[:half], turned[half:]
                out_ref[i, WIDE * p + e] = jnp.where(even, top, bottom)
                outgoing[r, WIDE * p + e] = jnp.where(even, bottom, top)

        @pl.when(r > 0)
        def _():
            send_row(r - 1).start()

    send_row(rows_here - 1).start()

    @pl.loop(0, rows_here)
    def _(r):
        send_row(r).wait()


def step(cap, ident, slots, kept, size):
    span = ROWS * slots
    chunks = len(pieces(cap))
    return pl.pallas_call(
        functools.partial(step_kernel, cap, slots, kept),
        out_shape=jax.ShapeDtypeStruct((ROWS, kept, size // 2, size), jnp.bfloat16),
        in_specs=[pl.BlockSpec(memory_space=pltpu.SMEM)]
        + [pl.BlockSpec(memory_space=pl.ANY)] * 3,
        out_specs=pl.BlockSpec(memory_space=pltpu.VMEM),
        scratch_shapes=[
            pltpu.VMEM((3 * span + 1, size, size), jnp.bfloat16),
            pltpu.VMEM((kept // WIDE, size, WIDE * size), jnp.float32),
            pltpu.VMEM((kept // WIDE, size, WIDE * size), jnp.bfloat16),
            pltpu.VMEM((ROWS // 2, kept, size // 2, size), jnp.bfloat16),
            pltpu.SemaphoreType.DMA((3,)),
            pltpu.SemaphoreType.DMA((2 * chunks,)),
            pltpu.SemaphoreType.DMA((2 * chunks,)),
            pltpu.SemaphoreType.DMA((2 * chunks,)),
            pltpu.SemaphoreType.DMA((2 * chunks,)),
            pltpu.SemaphoreType.DMA((ROWS // 2,)),
            pltpu.SemaphoreType.DMA((ROWS // 2,)),
        ],
        compiler_params=pltpu.CompilerParams(
            collective_id=ident,
            has_side_effects=True,
            vmem_limit_bytes=40 * 2**20,
        ),
        name="step_%d" % cap,
    )


CAPS = (54, 56, 58, 60, 62, 64, 72, 96)


def pieces(cap):
    return [cap - 20, 14, 6]


def local(blocks, cols, res):
    rows, slots, edge, size = blocks.shape
    kept = res.shape[1]
    span = rows * slots
    meta = pl.pallas_call(
        index_kernel,
        out_shape=jax.ShapeDtypeStruct((META_ROWS, LANES), jnp.int32),
        name="index",
    )(cols.T, res.T)
    flat = meta.reshape(-1)
    own = blocks.reshape(span, edge, size)
    up, down = pl.pallas_call(
        functools.partial(pack_kernel, slots),
        out_shape=[jax.ShapeDtypeStruct((span + 1, edge, size), blocks.dtype)] * 2,
        in_specs=[
            pl.BlockSpec(memory_space=pltpu.SMEM),
            pl.BlockSpec(memory_space=pltpu.VMEM),
        ],
        name="pack",
    )(flat, own)
    which = meta[COUNT, 0]
    packed = lax.switch(
        which,
        [step(cap, n, slots, kept, size) for n, cap in enumerate(CAPS)],
        flat,
        own,
        up,
        down,
    )
    return jnp.swapaxes(packed, 2, 3)


def solution(mesh):
    return jax.shard_map(
        local,
        mesh=mesh,
        in_specs=(P(("row", "col"), None, "depth", None), P(), P()),
        out_specs=P(("row", "col"), None, None, "depth"),
        check_vma=False,
    )
```

```python
import functools

import jax
import jax.numpy as jnp
from jax import lax
from jax.experimental import pallas as pl
from jax.experimental.pallas import tpu as pltpu
from jax.sharding import PartitionSpec as P

W = 8
ROWS = 8
LANES = 128
WIDE = 4
MESH = pl.DeviceIdType.MESH
OWN_COLS, OWN_RES, UP_SLOT, DOWN_SLOT, COUNT, META_ROWS = 40, 56, 72, 88, 104, 112


def group_index():
    return lax.axis_index("row") * lax.axis_size("col") + lax.axis_index("col")


def index_kernel(cols_ref, res_ref, meta_ref):
    slots, count = cols_ref.shape
    slots_kept = res_ref.shape[0]
    cols = cols_ref[...]
    res = res_ref[...]
    row = lax.broadcasted_iota(jnp.int32, (slots, count), 1)
    half = count // 2

    def offset(values):
        t = values - row
        t = jnp.where(t > half, t - count, t)
        return jnp.where(t < -half, t + count, t)

    present = cols >= 0
    off = offset(cols)
    in_group = row & (ROWS - 1)
    lane_group = in_group[:1]
    away = 4 * W
    off = jnp.where(present, off, away)
    extra = jnp.full((16 - slots, count), away, jnp.int32)
    off_all = jnp.concatenate([off, extra], axis=0)
    kept_all = jnp.concatenate([offset(res), extra], axis=0)

    def needed(sign):
        need = jnp.zeros((slots, count), jnp.int32)
        for d in range(1, W + 1):
            step = sign * d
            turn = count - d if sign > 0 else d
            kept_there = pltpu.roll(kept_all, turn, 1)
            off_there = pltpu.roll(off_all, turn, 1)
            reads = (kept_there == -step) | (off_there == -step)
            reads = jnp.max(jnp.where(reads, 1, 0), axis=0, keepdims=True)
            if sign > 0:
                inside = lane_group + d >= ROWS
            else:
                inside = lane_group - d < 0
            reads = jnp.where(inside, reads, 0)
            hit = jnp.zeros((slots, count), jnp.int32)
            for q in range(slots_kept):
                hit = jnp.where(off - step == kept_there[q : q + 1], 1, hit)
            need = jnp.maximum(need, hit * reads)
        return present & (need > 0)

    need_up = needed(1)
    need_down = needed(-1)

    def positions(need):
        ones = jnp.where(need, 1, 0)
        run = jnp.zeros((1, count), jnp.int32)
        within = []
        for s in range(slots):
            within.append(run)
            run = run + ones[s : s + 1]
        before = jnp.zeros((1, count), jnp.int32)
        wide = jnp.broadcast_to(run, (8, count))
        for j in range(1, ROWS):
            before = before + jnp.where(lane_group >= j, pltpu.roll(wide, j, 1)[:1], 0)
        return jnp.concatenate([w + before for w in within], axis=0), before + run

    pos_up, total_up = positions(need_up)
    pos_down, total_down = positions(need_down)
    most = jnp.max(jnp.maximum(total_up, total_down))
    which = jnp.int32(0)
    for cap in CAPS[:-1]:
        which = which + jnp.where(most > cap, 1, 0)

    first = group_index() * ROWS
    shift = lax.rem(count - first + ROWS, count)

    def window(values):
        padded = jnp.concatenate(
            [values, jnp.zeros((16 - slots, count), jnp.int32)], axis=0
        )
        return pltpu.roll(padded, shift, 1)[:, :LANES]

    span = ROWS * slots
    empty = 3 * span
    lane = lax.broadcasted_iota(jnp.int32, (16, LANES), 1)
    slot = lax.broadcasted_iota(jnp.int32, (16, LANES), 0)
    up_slot = window(jnp.where(need_up, pos_up, span))
    down_slot = window(jnp.where(need_down, pos_down, span))
    off_w = window(off)
    here = off_w < 4 * W
    place = jnp.where(
        lane < ROWS,
        jnp.where(up_slot < span, span + up_slot, empty),
        jnp.where(
            lane < 2 * ROWS,
            (lane - ROWS) * slots + slot,
            jnp.where(down_slot < span, 2 * span + down_slot, empty),
        ),
    )
    place = jnp.where(here & (lane < 3 * ROWS), place, empty)
    wanted = lax.broadcasted_iota(jnp.int32, (OWN_COLS, LANES), 0) - 2 * W
    dense = jnp.full((OWN_COLS, LANES), empty, jnp.int32)
    for s in range(slots):
        dense = jnp.where(off_w[s : s + 1] == wanted, place[s : s + 1], dense)
    meta_ref[:OWN_COLS] = dense
    reach_col = off_w + lane
    meta_ref[OWN_COLS:OWN_RES] = jnp.where(
        here, (2 * W - reach_col) * LANES + reach_col, LANES - 1
    )
    meta_ref[OWN_RES:UP_SLOT] = window(offset(res)) + lane
    meta_ref[UP_SLOT:DOWN_SLOT] = up_slot
    meta_ref[DOWN_SLOT:COUNT] = down_slot
    meta_ref[COUNT:] = jnp.full((META_ROWS - COUNT, LANES), which, jnp.int32)


def pack_kernel(slots, meta_ref, blocks_ref, up_ref, down_ref):
    @pl.loop(0, slots)
    def _(s):
        for u in range(ROWS):
            block = blocks_ref[u * slots + s]
            up_ref[meta_ref[(UP_SLOT + s) * LANES + ROWS + u]] = block
            down_ref[meta_ref[(DOWN_SLOT + s) * LANES + ROWS + u]] = block


def step_kernel(
    cap,
    slots,
    kept,
    meta_ref,
    blocks_ref,
    up_ref,
    down_ref,
    out_ref,
    table,
    square,
    rounded,
    outgoing,
    own_sem,
    send_sem,
    recv_sem,
    pass_send_sem,
    pass_recv_sem,
    out_send_sem,
    out_recv_sem,
):
    row, col, depth = (lax.axis_index(a) for a in ("row", "col", "depth"))
    row_count, col_count = lax.axis_size("row"), lax.axis_size("col")
    groups = row_count * col_count
    group = row * col_count + col
    following = lax.rem(group + 1, groups)
    preceding = lax.rem(group + groups - 1, groups)
    sibling = (row, col, 1 - depth)
    after = (following // col_count, lax.rem(following, col_count), depth)
    before = (preceding // col_count, lax.rem(preceding, col_count), depth)

    barrier = pltpu.get_barrier_semaphore()
    for device in (sibling, after, before):
        pl.semaphore_signal(barrier, inc=1, device_id=device, device_id_type=MESH)
    pl.semaphore_wait(barrier, 3)

    span = ROWS * slots
    edge = blocks_ref.shape[1]
    mine = pl.ds(pl.multiple_of(depth * edge, edge), edge)

    halo = []
    done = 0
    for c, part in enumerate(pieces(cap)):
        for way, (source, device) in enumerate(((up_ref, after), (down_ref, before))):
            start = span * (way + 1) + done
            k = 2 * c + way
            copy = pltpu.make_async_remote_copy(
                src_ref=source.at[pl.ds(done, part)],
                dst_ref=table.at[pl.ds(start, part), mine, :],
                send_sem=send_sem.at[k],
                recv_sem=recv_sem.at[k],
                device_id=device,
                device_id_type=MESH,
            )
            copy.start()
            halo.append((k, start, part, copy))
        done += part
    keep = pltpu.make_async_copy(
        blocks_ref, table.at[pl.ds(0, span), mine, :], own_sem.at[0]
    )
    keep.start()
    share = pltpu.make_async_remote_copy(
        src_ref=blocks_ref,
        dst_ref=table.at[pl.ds(0, span), mine, :],
        send_sem=own_sem.at[1],
        recv_sem=own_sem.at[2],
        device_id=sibling,
        device_id_type=MESH,
    )
    share.start()
    table[3 * span] = jnp.zeros(table.shape[1:], table.dtype)
    passed = []
    for k, start, part, copy in halo:
        copy.wait_recv()
        forward = pltpu.make_async_remote_copy(
            src_ref=table.at[pl.ds(start, part), mine, :],
            dst_ref=table.at[pl.ds(start, part), mine, :],
            send_sem=pass_send_sem.at[k],
            recv_sem=pass_recv_sem.at[k],
            device_id=sibling,
            device_id_type=MESH,
        )
        forward.start()
        passed.append(forward)
    keep.wait()
    share.wait()
    for forward in passed:
        forward.wait()
    for _, _, _, copy in halo:
        copy.wait_send()

    rows_here = ROWS // 2
    size = table.shape[2]
    even = depth == 0
    half = size // 2

    def right(bases, to):
        return jnp.concatenate(
            [
                jnp.concatenate([table[meta_ref[b + t]] for t in to], axis=1)
                for b in bases
            ],
            axis=0,
        )

    def send_row(r):
        return pltpu.make_async_remote_copy(
            src_ref=outgoing.at[r],
            dst_ref=out_ref.at[depth * rows_here + r],
            send_sem=out_send_sem.at[r],
            recv_sem=out_recv_sem.at[r],
            device_id=sibling,
            device_id_type=MESH,
        )

    @pl.loop(0, rows_here)
    def _(r):
        i = depth * rows_here + r

        def targets(p):
            return [
                meta_ref[(OWN_RES + WIDE * p + e) * LANES + ROWS + i] * LANES
                for e in range(WIDE)
            ]

        @pl.loop(0, kept // WIDE)
        def _(p):
            to = targets(p)
            total = jnp.zeros((size, WIDE * size), jnp.float32)
            for s in range(0, slots, 2):
                left = jnp.concatenate(
                    [table[i * slots + s], table[i * slots + s + 1]], axis=1
                )
                bases = [
                    meta_ref[(OWN_COLS + s + e) * LANES + ROWS + i] for e in range(2)
                ]
                total = total + jnp.dot(
                    left, right(bases, to), preferred_element_type=jnp.float32
                )
            square[p] = total
            rounded[p] = total.astype(jnp.bfloat16)

        @pl.loop(0, kept // WIDE)
        def _(p):
            to = targets(p)
            total = jnp.zeros((size, WIDE * size), jnp.float32)
            for q in range(0, kept, 2):
                bases = [
                    2 * W * LANES
                    - (LANES - 1) * meta_ref[(OWN_RES + q + e) * LANES + ROWS + i]
                    for e in range(2)
                ]
                at = q % WIDE * size
                total = total + jnp.dot(
                    rounded[q // WIDE, :, at : at + 2 * size],
                    right(bases, to),
                    preferred_element_type=jnp.float32,
                )
            value = (3.0 * square[p] - 2.0 * total).astype(jnp.bfloat16)
            for e in range(WIDE):
                turned = value[:, e * size : (e + 1) * size].T
                top, bottom = turned[:half], turned[half:]
                out_ref[i, WIDE * p + e] = jnp.where(even, top, bottom)
                outgoing[r, WIDE * p + e] = jnp.where(even, bottom, top)

        @pl.when(r > 0)
        def _():
            send_row(r - 1).start()

    send_row(rows_here - 1).start()

    @pl.loop(0, rows_here)
    def _(r):
        send_row(r).wait()


def step(cap, ident, slots, kept, size):
    span = ROWS * slots
    chunks = len(pieces(cap))
    return pl.pallas_call(
        functools.partial(step_kernel, cap, slots, kept),
        out_shape=jax.ShapeDtypeStruct((ROWS, kept, size // 2, size), jnp.bfloat16),
        in_specs=[pl.BlockSpec(memory_space=pltpu.SMEM)]
        + [pl.BlockSpec(memory_space=pl.ANY)] * 3,
        out_specs=pl.BlockSpec(memory_space=pltpu.VMEM),
        scratch_shapes=[
            pltpu.VMEM((3 * span + 1, size, size), jnp.bfloat16),
            pltpu.VMEM((kept // WIDE, size, WIDE * size), jnp.float32),
            pltpu.VMEM((kept // WIDE, size, WIDE * size), jnp.bfloat16),
            pltpu.VMEM((ROWS // 2, kept, size // 2, size), jnp.bfloat16),
            pltpu.SemaphoreType.DMA((3,)),
            pltpu.SemaphoreType.DMA((2 * chunks,)),
            pltpu.SemaphoreType.DMA((2 * chunks,)),
            pltpu.SemaphoreType.DMA((2 * chunks,)),
            pltpu.SemaphoreType.DMA((2 * chunks,)),
            pltpu.SemaphoreType.DMA((ROWS // 2,)),
            pltpu.SemaphoreType.DMA((ROWS // 2,)),
        ],
        compiler_params=pltpu.CompilerParams(
            collective_id=ident,
            has_side_effects=True,
            vmem_limit_bytes=40 * 2**20,
        ),
        name="step_%d" % cap,
    )


CAPS = (54, 56, 58, 60, 62, 64, 68, 96)


def pieces(cap):
    return [(cap + k) // 4 for k in range(4)]


def local(blocks, cols, res):
    rows, slots, edge, size = blocks.shape
    kept = res.shape[1]
    span = rows * slots
    meta = pl.pallas_call(
        index_kernel,
        out_shape=jax.ShapeDtypeStruct((META_ROWS, LANES), jnp.int32),
        name="index",
    )(cols.T, res.T)
    flat = meta.reshape(-1)
    own = blocks.reshape(span, edge, size)
    up, down = pl.pallas_call(
        functools.partial(pack_kernel, slots),
        out_shape=[jax.ShapeDtypeStruct((span + 1, edge, size), blocks.dtype)] * 2,
        in_specs=[
            pl.BlockSpec(memory_space=pltpu.SMEM),
            pl.BlockSpec(memory_space=pltpu.VMEM),
        ],
        name="pack",
    )(flat, own)
    which = meta[COUNT, 0]
    packed = lax.switch(
        which,
        [step(cap, n, slots, kept, size) for n, cap in enumerate(CAPS)],
        flat,
        own,
        up,
        down,
    )
    return jnp.swapaxes(packed, 2, 3)


def solution(mesh):
    return jax.shard_map(
        local,
        mesh=mesh,
        in_specs=(P(("row", "col"), None, "depth", None), P(), P()),
        out_specs=P(("row", "col"), None, None, "depth"),
        check_vma=False,
    )
```
